256 devices in a mesh: section: 8 (over x, core), seq: 32 (over z, y).
Axes of the slice: x: 4, y: 4, z: 8, core: 2. Of those that a mesh axis runs over, the one named last changes fastest.
Arguments:
- queries: bfloat16 [8, 10240, 4096], P('section', 'seq'), may hold values from -60 to 60
- keys_new: bfloat16 [8, 10240, 4096], P('section', 'seq'), may hold values from -6 to 6
- values_new: bfloat16 [8, 10240, 4096], P('section', 'seq'), may hold values from -6 to 6
- keys_cache: bfloat16 [8, 6144, 4096], P('section', None, 'seq'), may hold values from -6 to 6
- values_cache: bfloat16 [8, 6144, 4096], P('section', None, 'seq'), may hold values from -6 to 6
- window: int32 [8, 32], P('section', 'seq'), may hold values from 1 to 3, as said below
- global_blocks: int32 [8, 2], P('section'), may hold values from 0 to 95
- random_blocks: int32 [8, 160, 3], P('section'), may hold values from 0 to 95
Outputs:
- handed: bfloat16 [8, 10240, 4096], P('section', 'seq')
The draws below stay inside these ranges and needn't reach their ends.
Inputs may be any that keep to these rules, and one draw needn't show every extreme that they name: In every section some head has the window 3.
All inputs are finite; a program needn't handle non-finite values.
Results may differ from the reference program's by a relative error of at most 0.0049.
Values may be sent and summed in bfloat16 or wider, within the bound.
A program may use at most 128 MiB of HBM per device.

```python
import math
import jax
import jax.numpy as jnp
from jax import lax

HD = 128
HEADS = 32
WIDE = 4096
BLK = 64
WMAX = 3
GLOB = 2
RAND = 3
NK = 8
CTXB = 96
SECTIONS = 8
STRETCH = 10240
QBLK = 160
CTX = 6144


def aligned_pair(key):
    base = jax.random.fold_in(key, 7)
    shape = (SECTIONS, STRETCH, WIDE)
    keys = jnp.clip(jax.random.normal(jax.random.fold_in(base, 1), shape, jnp.float32), -6.0, 6.0)
    queries = jnp.clip(jax.random.normal(jax.random.fold_in(base, 2), shape, jnp.float32), -6.0, 6.0)
    token_at = jnp.arange(STRETCH)[None, :, None]
    column_at = jnp.arange(WIDE)[None, None, :]
    upper_end = (token_at == 0) & (column_at == 0)
    lower_end = (token_at == 1) & (column_at == 0)
    queries = jnp.where(upper_end, 60.0, jnp.where(lower_end, -60.0, queries))
    keys = jnp.where(upper_end, 6.0, jnp.where(lower_end, -6.0, keys))
    return (queries, keys)


def draw_queries(key, part):
    return aligned_pair(key)[0].astype(jnp.bfloat16)


def draw_keys_new(key, part):
    return aligned_pair(key)[1].astype(jnp.bfloat16)


def draw_window(key, part):
    spans = jax.random.randint(jax.random.fold_in(key, 3), (SECTIONS, HEADS), 1, WMAX + 1)
    chosen = jax.random.randint(jax.random.fold_in(key, 4), (SECTIONS, 1), 0, HEADS)
    return jnp.where(jnp.arange(HEADS)[None, :] == chosen, WMAX, spans).astype(jnp.int32)


def place_ends(entries, stream_key, least, high):
    extent = entries.shape
    place = [jax.random.randint(jax.random.fold_in(stream_key, axis), (), 0, extent[axis]) for axis in range(len(extent))]
    entries = entries.at[tuple(place)].set(least)
    longest = extent.index(max(extent))
    place[longest] = (place[longest] + 1) % extent[longest]
    return entries.at[tuple(place)].set(high)


def levels(stream_key, shape, split, smallest, largest):
    gain = 1.0
    for axis_at, parts in split:
        draws = jax.random.uniform(jax.random.fold_in(jax.random.fold_in(stream_key, 6), axis_at), (parts,), jnp.float32, smallest / len(split), largest / len(split))
        gain = gain * jnp.repeat(jnp.exp(draws), shape[axis_at] // parts).reshape((-1,) + (1,) * (len(shape) - 1 - axis_at))
    return gain


def bell_draw(rng, shape, width, reach, cuts=(), held_as=jnp.bfloat16):
    factor_of = levels(rng, shape, cuts, -0.22, 0.18) if cuts else 1.0
    drawn = jax.random.normal(rng, shape, jnp.float32) * width * factor_of
    return jnp.minimum(jnp.maximum(drawn, -reach), reach).astype(held_as)


def setup_inputs(seed: int = 0) -> dict:
    splits = jax.random.split(jax.random.key(seed), 9)
    queries = draw_queries(jax.random.fold_in(splits[8], 71), 0)
    keys_new = draw_keys_new(jax.random.fold_in(splits[8], 71), 0)
    values_new = bell_draw(splits[2], (SECTIONS, STRETCH, WIDE), 1.0, 6.0, ((0, 8), (1, 32)))
    keys_cache = bell_draw(splits[3], (SECTIONS, CTX, WIDE), 1.0, 6.0, ((0, 8), (2, 32)))
    values_cache = bell_draw(splits[4], (SECTIONS, CTX, WIDE), 1.0, 6.0, ((0, 8), (2, 32)))
    window = draw_window(jax.random.fold_in(splits[8], 71), 0)
    global_blocks = place_ends(jax.random.randint(splits[6], (SECTIONS, GLOB), 0, CTXB), jax.random.fold_in(splits[6], 1), 0, CTXB - 1).astype(jnp.int32)
    random_blocks = place_ends(jax.random.randint(splits[7], (SECTIONS, QBLK, RAND), 0, CTXB), jax.random.fold_in(splits[7], 1), 0, CTXB - 1).astype(jnp.int32)
    return dict(queries=queries, keys_new=keys_new, values_new=values_new, keys_cache=keys_cache, values_cache=values_cache, window=window, global_blocks=global_blocks, random_blocks=random_blocks)


masked_score = -1e+30

def block_mask(span_blocks):
    rows = jnp.arange(BLK, dtype=jnp.int32)[:, None]
    column = jnp.arange(NK * BLK, dtype=jnp.int32)[None, :]
    which = column // BLK
    inside = column % BLK
    allowed = jnp.where(which >= WMAX, True, which < span_blocks)
    return allowed & ((which != 0) | (inside <= rows))

def attend_head(query, key_all, value_all, span_blocks, table):
    query_blocks = query.reshape(QBLK, BLK, HD).astype(jnp.float32)
    key_blocks = key_all.reshape(CTXB + QBLK, BLK, HD)
    value_blocks = value_all.reshape(CTXB + QBLK, BLK, HD)
    picked_keys = key_blocks[table].reshape(QBLK, NK * BLK, HD).astype(jnp.float32)
    picked_values = value_blocks[table].reshape(QBLK, NK * BLK, HD).astype(jnp.float32)
    scores = jnp.einsum('qih,qjh->qij', query_blocks, picked_keys) * (1.0 / math.sqrt(HD))
    scores = jnp.where(block_mask(span_blocks)[None], scores, masked_score)
    top = lax.optimization_barrier(jnp.max(scores, axis=-1, keepdims=True))
    expo = jnp.exp(scores - top)
    weights = (expo / lax.optimization_barrier(jnp.sum(expo, axis=-1, keepdims=True))).astype(jnp.bfloat16)
    result = jnp.einsum('qij,qjh->qih', weights.astype(jnp.float32), picked_values)
    return result.astype(jnp.bfloat16).reshape(STRETCH, HD)

def reference(queries, keys_new, values_new, keys_cache, values_cache, window, global_blocks, random_blocks):
    zero = jnp.int32(0)

    def one_item(item):
        section_at = item // HEADS
        head_at = item % HEADS
        column = head_at * HD
        query = lax.dynamic_slice(queries, (section_at, zero, column), (1, STRETCH, HD))[0]
        fresh_keys = lax.dynamic_slice(keys_new, (section_at, zero, column), (1, STRETCH, HD))[0]
        fresh_values = lax.dynamic_slice(values_new, (section_at, zero, column), (1, STRETCH, HD))[0]
        old_keys = lax.dynamic_slice(keys_cache, (section_at, zero, column), (1, CTX, HD))[0]
        old_values = lax.dynamic_slice(values_cache, (section_at, zero, column), (1, CTX, HD))[0]
        key_all = jnp.concatenate([old_keys, fresh_keys], axis=0)
        value_all = jnp.concatenate([old_values, fresh_values], axis=0)
        span_blocks = lax.dynamic_slice(window, (section_at, head_at), (1, 1))[0, 0]
        global_row = lax.dynamic_slice(global_blocks, (section_at, zero), (1, GLOB))[0]
        random_rows = lax.dynamic_slice(random_blocks, (section_at, zero, zero), (1, QBLK, RAND))[0]
        starts = CTXB + jnp.arange(QBLK, dtype=jnp.int32)[:, None] - jnp.arange(WMAX, dtype=jnp.int32)[None, :]
        spread = jnp.broadcast_to(global_row[None, :], (QBLK, GLOB)).astype(jnp.int32)
        table = jnp.concatenate([starts, spread, random_rows.astype(jnp.int32)], axis=1)
        return attend_head(query, key_all, value_all, span_blocks, table)
    outputs = lax.map(one_item, jnp.arange(SECTIONS * HEADS, dtype=jnp.int32))
    outputs = outputs.reshape(SECTIONS, HEADS, STRETCH, HD).transpose(0, 2, 1, 3).reshape(SECTIONS, STRETCH, WIDE)
    return jnp.roll(outputs, 1, axis=0)
```

```python
import functools
import math

import jax
import jax.numpy as jnp
from jax import lax
from jax.experimental import pallas as pl
from jax.experimental.pallas import tpu as pltpu
from jax.sharding import PartitionSpec as P

HD = 128
BLK = 64
WMAX = 3
GLOB = 2
RAND = 3
LEAD = (WMAX - 1) * BLK
STAT = 16

MESH = pl.DeviceIdType.MESH
SCALE2 = math.log2(math.e) / math.sqrt(HD)
MASKED = -1e30


def signed_step(j, size):
    half = lax.div(j + 1, 2)
    odd = lax.rem(j, 2)
    return lax.rem(half * (2 * odd - 1) + size, size)


def nt_dot(a, b):
    return lax.dot_general(a, b, (((1,), (1,)), ((), ())), preferred_element_type=jnp.float32)


def kernel(
    n,
    ny,
    sections,
    q_hbm,
    k_hbm,
    v_hbm,
    kc_hbm,
    vc_hbm,
    win_ref,
    glob_ref,
    rand_ref,
    out_hbm,
    qv,
    kall,
    vall,
    kcv,
    vcv,
    qbuf,
    obuf,
    ogbuf,
    owbuf,
    lwbuf,
    fbuf,
    wbuf,
    thr,
    loc_sem,
    qrecv,
    orecv,
    qsend,
    osend,
    fsend,
    frecv,
    wsend,
    wrecv,
    hrecv,
    hsend,
    tsend,
):
    nz = n // ny
    rows = q_hbm.shape[1]
    cached = kc_hbm.shape[1]
    nb = rows // BLK
    sec = lax.axis_index("section")
    me = lax.axis_index("seq")
    z, y = lax.div(me, ny), lax.rem(me, ny)

    def at(i, back):
        dz = signed_step(lax.rem(i, nz), nz)
        dy = signed_step(lax.div(i, nz), ny)
        if back:
            dz, dy = nz - dz, ny - dy
        return lax.rem(z + dz, nz) * ny + lax.rem(y + dy, ny)

    def peer(i):
        return at(i, False)

    def source(i):
        return at(i, True)

    def columns(h):
        return pl.ds(pl.multiple_of(h * HD, HD), HD)

    def remote(src, dst, send, recv, seq, section=None):
        where = {"section": sec if section is None else section, "seq": seq}
        return pltpu.make_async_remote_copy(
            src_ref=src, dst_ref=dst, send_sem=send, recv_sem=recv, device_id=where, device_id_type=MESH
        )

    after = lax.rem(sec + 1, sections)
    before = lax.rem(sec + sections - 1, sections)

    local = [
        pltpu.make_async_copy(q_hbm.at[0], qv, loc_sem.at[0]),
        pltpu.make_async_copy(k_hbm.at[0], kall.at[pl.ds(LEAD, rows)], loc_sem.at[1]),
        pltpu.make_async_copy(v_hbm.at[0], vall.at[pl.ds(LEAD, rows)], loc_sem.at[2]),
        pltpu.make_async_copy(kc_hbm.at[0], kcv, loc_sem.at[3]),
        pltpu.make_async_copy(vc_hbm.at[0], vcv, loc_sem.at[4]),
    ]
    for copy in local:
        copy.start()
    pltpu.make_async_copy(q_hbm.at[0, :, columns(me)], qbuf.at[0], qrecv.at[0]).start()

    wbuf[0] = jnp.full((8, HD), win_ref[0, 0].astype(jnp.float32))

    barrier = pltpu.get_barrier_semaphore()

    def greet(i, carry):
        pl.semaphore_signal(barrier, 1, device_id={"section": sec, "seq": peer(i)}, device_id_type=MESH)
        return carry

    lax.fori_loop(1, n, greet, 0)
    for other in (after, before):
        pl.semaphore_signal(barrier, 1, device_id={"section": other, "seq": me}, device_id_type=MESH)
    pl.semaphore_wait(barrier, n + 1)

    def send_queries(i, carry):
        p = peer(i)
        remote(wbuf.at[0], wbuf.at[i], wsend, wrecv, p).start()
        remote(q_hbm.at[0, :, columns(p)], qbuf.at[i], qsend, qrecv.at[i], p).start()
        return carry

    lax.fori_loop(1, n, send_queries, 0)

    halo = []
    tail = []
    own_tail = []
    for j, (fresh, cache, whole) in enumerate(((k_hbm, kc_hbm, kall), (v_hbm, vc_hbm, vall))):
        halo.append(
            remote(
                fresh.at[0, pl.ds(rows - LEAD, LEAD)],
                whole.at[pl.ds(0, LEAD)],
                hsend.at[j],
                hrecv.at[j],
                lax.rem(me + 1, n),
            )
        )
        for w in range(WMAX - 1):
            block = cache.at[0, cached - WMAX + 1 + w]
            place = pl.ds(w * BLK, BLK)
            tail.append(
                remote(block, whole.at[place, columns(me)], tsend.at[j, w], hrecv.at[j], 0)
            )
            own_tail.append(
                pltpu.make_async_copy(block, whole.at[place, pl.ds(0, HD)], hrecv.at[j])
            )

    @pl.when(me < n - 1)
    def _():
        for copy in halo:
            copy.start()

    @pl.when(me > 0)
    def _():
        for copy in tail:
            copy.start()

    @pl.when(me == 0)
    def _():
        for copy in own_tail:
            copy.start()

    row = lax.broadcasted_iota(jnp.int32, (BLK, WMAX * BLK), 0)
    col = lax.broadcasted_iota(jnp.int32, (BLK, WMAX * BLK), 1)
    late = col - (WMAX - 1) * BLK > row
    width = jnp.where(col < BLK, 3.0, jnp.where(col < 2 * BLK, 2.0, jnp.where(late, 99.0, 1.0)))
    thr[...] = width

    def window_part(i, blocks):
        h = source(i)
        span = wbuf[i, 0:1, 0:1]
        allowed = thr[...] <= span
        for b in blocks:
            q = qv[b * BLK : (b + 1) * BLK, columns(h)]
            k = kall[b * BLK : b * BLK + WMAX * BLK, columns(h)]
            v = vall[b * BLK : b * BLK + WMAX * BLK, columns(h)]
            s = jnp.where(allowed, nt_dot(q, k), MASKED)
            top = jnp.max(s, axis=1, keepdims=True)
            e = jnp.exp2((s - top) * SCALE2)
            total = jnp.sum(e, axis=1, keepdims=True)
            o = jnp.dot(e.astype(jnp.bfloat16), v, preferred_element_type=jnp.float32)
            owbuf[h, b * BLK : (b + 1) * BLK, :] = o / total
            lwbuf[h, b * BLK : (b + 1) * BLK, :] = jnp.broadcast_to(
                top * SCALE2 + jnp.log2(total), (BLK, HD)
            )

    def inner_window(i, carry):
        window_part(i, range(WMAX - 1, nb))
        return carry

    def edge_window(i, carry):
        window_part(i, range(WMAX - 1))
        return carry

    for copy in local[:3]:
        copy.wait()
    pltpu.make_async_copy(wbuf.at[pl.ds(1, n - 1)], wbuf.at[pl.ds(1, n - 1)], wrecv).wait()
    lax.fori_loop(0, n, inner_window, 0)

    for copy in local[3:]:
        copy.wait()

    diagonal = lax.broadcasted_iota(jnp.int32, (BLK, HD), 0) == lax.broadcasted_iota(
        jnp.int32, (BLK, HD), 1
    )
    stat_row = lax.broadcasted_iota(jnp.int32, (STAT, HD), 0)

    def far_part(i, carry):
        src = source(i)
        pltpu.make_async_copy(qbuf.at[i], qbuf.at[i], qrecv.at[i]).wait()
        stats = jnp.zeros((STAT, HD), jnp.float32)
        for b in range(nb):
            picks = [glob_ref[0, g] for g in range(GLOB)] + [
                rand_ref[0, src * nb + b, r] for r in range(RAND)
            ]
            k = jnp.concatenate([kcv[x] for x in picks], axis=0)
            v = jnp.concatenate([vcv[x] for x in picks], axis=0)
            s = nt_dot(qbuf[i, b * BLK : (b + 1) * BLK, :], k)
            top = jnp.max(s, axis=1, keepdims=True)
            e = jnp.exp2((s - top) * SCALE2)
            total = jnp.sum(e, axis=1, keepdims=True)
            o = jnp.dot(e.astype(jnp.bfloat16), v, preferred_element_type=jnp.float32)
            obuf[i, b * BLK : (b + 1) * BLK, :] = (o / total).astype(jnp.bfloat16)
            lse = top * SCALE2 + jnp.log2(total)
            line = jnp.sum(jnp.where(diagonal, lse, 0.0), axis=0, keepdims=True)
            for part in range(3):
                piece = line.astype(jnp.bfloat16).astype(jnp.float32)
                stats = jnp.where(stat_row == part * nb + b, piece, stats)
                line = line - piece
        obuf[i, nb * BLK : nb * BLK + STAT, :] = stats.astype(jnp.bfloat16)

        @pl.when(i > 0)
        def _():
            remote(obuf.at[i], ogbuf.at[i], osend, orecv.at[i], src).start()

        @pl.when(i == 0)
        def _():
            pltpu.make_async_copy(obuf.at[i], ogbuf.at[i], orecv.at[i]).start()

        return carry

    lax.fori_loop(0, n, far_part, 0)

    for j, whole in enumerate((kall, vall)):
        pltpu.make_async_copy(whole.at[pl.ds(0, LEAD)], whole.at[pl.ds(0, LEAD)], hrecv.at[j]).wait()
    lax.fori_loop(0, n, edge_window, 0)

    def join(i, carry):
        h = peer(i)
        pltpu.make_async_copy(ogbuf.at[i], ogbuf.at[i], orecv.at[i]).wait()
        stats = ogbuf[i, nb * BLK : nb * BLK + STAT, :].astype(jnp.float32)
        for b in range(nb):
            line = (stats[b : b + 1] + stats[nb + b : nb + b + 1]) + stats[2 * nb + b : 2 * nb + b + 1]
            far = jnp.sum(jnp.where(diagonal, line, 0.0), axis=1, keepdims=True)
            near = lwbuf[h, b * BLK : (b + 1) * BLK, :]
            share = 1.0 / (1.0 + jnp.exp2(near - far))
            ow = owbuf[h, b * BLK : (b + 1) * BLK, :]
            og = ogbuf[i, b * BLK : (b + 1) * BLK, :].astype(jnp.float32)
            fbuf[i, b * BLK : (b + 1) * BLK, :] = (ow + share * (og - ow)).astype(jnp.bfloat16)
        remote(fbuf.at[i], out_hbm.at[0, :, columns(h)], fsend, frecv, me, after).start()
        return carry

    lax.fori_loop(0, n, join, 0)

    pltpu.make_async_copy(wbuf.at[pl.ds(1, n - 1)], wbuf.at[pl.ds(1, n - 1)], wsend).wait()
    pltpu.make_async_copy(qbuf.at[pl.ds(1, n - 1)], qbuf.at[pl.ds(1, n - 1)], qsend).wait()
    pltpu.make_async_copy(obuf.at[pl.ds(1, n - 1)], obuf.at[pl.ds(1, n - 1)], osend).wait()
    pltpu.make_async_copy(fbuf, fbuf, fsend).wait()
    pltpu.make_async_copy(out_hbm.at[0], out_hbm.at[0], frecv).wait()

    @pl.when(me < n - 1)
    def _():
        for copy in halo:
            copy.wait_send()

    @pl.when(me > 0)
    def _():
        for copy in tail:
            copy.wait_send()


def per_device(n, ny, sections, q, k, v, kc, vc, window, glob, rand):
    rows, wide = q.shape[1:]
    cached = kc.shape[1] // BLK
    kc, vc = (cache.reshape(1, cached, BLK, HD) for cache in (kc, vc))
    any_space = pl.BlockSpec(memory_space=pl.ANY)
    smem = pl.BlockSpec(memory_space=pltpu.SMEM)
    bf, f32, dma = jnp.bfloat16, jnp.float32, pltpu.SemaphoreType.DMA
    return pl.pallas_call(
        functools.partial(kernel, n, ny, sections),
        out_shape=jax.ShapeDtypeStruct(q.shape, bf),
        in_specs=[any_space] * 5 + [smem] * 3,
        out_specs=any_space,
        scratch_shapes=[
            pltpu.VMEM((rows, wide), bf),
            pltpu.VMEM((rows + LEAD, wide), bf),
            pltpu.VMEM((rows + LEAD, wide), bf),
            pltpu.VMEM((cached, BLK, HD), bf),
            pltpu.VMEM((cached, BLK, HD), bf),
            pltpu.VMEM((n, rows, HD), bf),
            pltpu.VMEM((n, rows + STAT, HD), bf),
            pltpu.VMEM((n, rows + STAT, HD), bf),
            pltpu.VMEM((n, rows, HD), f32),
            pltpu.VMEM((n, rows, HD), f32),
            pltpu.VMEM((n, rows, HD), bf),
            pltpu.VMEM((n, 8, HD), f32),
            pltpu.VMEM((BLK, WMAX * BLK), f32),
            dma((5,)),
            dma((n,)),
            dma((n,)),
            dma,
            dma,
            dma,
            dma,
            dma,
            dma,
            dma((2,)),
            dma((2,)),
            dma((2, WMAX - 1)),
        ],
        compiler_params=pltpu.CompilerParams(
            collective_id=0, has_side_effects=True, vmem_limit_bytes=56 * 1024 * 1024
        ),
    )(q, k, v, kc, vc, window, glob, rand)


def solution(mesh):
    n, sections = mesh.shape["seq"], mesh.shape["section"]
    ny = math.gcd(n, 4)
    placed = (
        P("section", "seq", None),
        P("section", "seq", None),
        P("section", "seq", None),
        P("section", None, "seq"),
        P("section", None, "seq"),
        P("section", "seq"),
        P("section", None),
        P("section", None, None),
    )
    return jax.shard_map(
        functools.partial(per_device, n, ny, sections),
        mesh=mesh,
        in_specs=placed,
        out_specs=P("section", "seq", None),
        check_vma=False,
    )
```

```python
import functools
import math

import jax
import jax.numpy as jnp
from jax import lax
from jax.experimental import pallas as pl
from jax.experimental.pallas import tpu as pltpu
from jax.sharding import PartitionSpec as P

HD = 128
BLK = 64
WMAX = 3
GLOB = 2
RAND = 3
LEAD = (WMAX - 1) * BLK
STAT = 16

MESH = pl.DeviceIdType.MESH
SCALE2 = math.log2(math.e) / math.sqrt(HD)
MASKED = -1e30


def signed_step(j, size):
    half = lax.div(j + 1, 2)
    odd = lax.rem(j, 2)
    return lax.rem(half * (2 * odd - 1) + size, size)


def nt_dot(a, b):
    return lax.dot_general(a, b, (((1,), (1,)), ((), ())), preferred_element_type=jnp.float32)


def kernel(
    n,
    ny,
    sections,
    q_hbm,
    k_hbm,
    v_hbm,
    kc_hbm,
    vc_hbm,
    win_ref,
    glob_ref,
    rand_ref,
    out_hbm,
    qv,
    kall,
    vall,
    kcv,
    vcv,
    qbuf,
    obuf,
    ogbuf,
    owbuf,
    lwbuf,
    fbuf,
    wbuf,
    relay,
    thr,
    loc_sem,
    qrecv,
    orecv,
    qsend,
    osend,
    fsend,
    frecv,
    wsend,
    wrecv,
    hrecv,
    hsend,
    tsend,
    rsend,
    rrecv,
):
    nz = n // ny
    rows = q_hbm.shape[1]
    cached = kc_hbm.shape[1]
    nb = rows // BLK
    sec = lax.axis_index("section")
    me = lax.axis_index("seq")
    z, y = lax.div(me, ny), lax.rem(me, ny)

    def at(i, back):
        dz = signed_step(lax.rem(i, nz), nz)
        dy = signed_step(lax.div(i, nz), ny)
        if back:
            dz, dy = nz - dz, ny - dy
        return lax.rem(z + dz, nz) * ny + lax.rem(y + dy, ny)

    def peer(i):
        return at(i, False)

    def source(i):
        return at(i, True)

    def columns(h):
        return pl.ds(pl.multiple_of(h * HD, HD), HD)

    def remote(src, dst, send, recv, seq, section=None):
        where = {"section": sec if section is None else section, "seq": seq}
        return pltpu.make_async_remote_copy(
            src_ref=src, dst_ref=dst, send_sem=send, recv_sem=recv, device_id=where, device_id_type=MESH
        )

    after = lax.rem(sec + 1, sections)
    before = lax.rem(sec + sections - 1, sections)

    local = [
        pltpu.make_async_copy(q_hbm.at[0], qv, loc_sem.at[0]),
        pltpu.make_async_copy(k_hbm.at[0], kall.at[pl.ds(LEAD, rows)], loc_sem.at[1]),
        pltpu.make_async_copy(v_hbm.at[0], vall.at[pl.ds(LEAD, rows)], loc_sem.at[2]),
        pltpu.make_async_copy(kc_hbm.at[0], kcv, loc_sem.at[3]),
        pltpu.make_async_copy(vc_hbm.at[0], vcv, loc_sem.at[4]),
    ]
    for copy in local:
        copy.start()
    pltpu.make_async_copy(q_hbm.at[0, :, columns(me)], qbuf.at[0], qrecv.at[0]).start()

    wbuf[me] = jnp.full((8, HD), win_ref[0, 0].astype(jnp.float32))

    barrier = pltpu.get_barrier_semaphore()

    def greet(i, carry):
        pl.semaphore_signal(barrier, 1, device_id={"section": sec, "seq": peer(i)}, device_id_type=MESH)
        return carry

    lax.fori_loop(1, n, greet, 0)
    for other in (after, before):
        pl.semaphore_signal(barrier, 1, device_id={"section": other, "seq": me}, device_id_type=MESH)
    pl.semaphore_wait(barrier, n + 1)

    wide = q_hbm.shape[2]
    quarter = wide // ny
    lead = pl.ds(0, LEAD)
    last = pl.ds(rows - LEAD, LEAD)
    fresh = (k_hbm, v_hbm)
    caches = (kc_hbm, vc_hbm)
    wholes = (kall, vall)
    edge = y == ny - 1
    ahead = z < nz - 1

    parts = n // 2
    piece = wide // parts
    per = parts // ny

    def send_window(i, carry):
        remote(wbuf.at[me], wbuf.at[me], wsend, wrecv, peer(i)).start()
        return carry

    def send_queries(i, carry):
        p = peer(i)
        remote(q_hbm.at[0, :, columns(p)], qbuf.at[i], qsend, qrecv.at[i], p).start()
        at_part = i - 1
        part = pl.ds(pl.multiple_of(at_part * piece, HD), piece)
        column = lax.div(at_part, per)
        by_relay = edge & (column < ny - 1)

        @pl.when((at_part < parts) & by_relay & ahead)
        def _():
            held = pl.ds(pl.multiple_of(lax.rem(at_part, per) * piece, HD), piece)
            for j in range(2):
                remote(
                    fresh[j].at[0, last, part], relay.at[j, :, held], rsend, rrecv, z * ny + column
                ).start()

        @pl.when((at_part < parts) & jnp.logical_not(by_relay) & (me < n - 1))
        def _():
            for j in range(2):
                remote(
                    fresh[j].at[0, last, part], wholes[j].at[lead, part], hsend.at[j], hrecv.at[j], me + 1
                ).start()

        return carry

    head_start = min(5, n)
    lax.fori_loop(1, head_start, send_queries, 0)
    lax.fori_loop(1, n, send_window, 0)
    lax.fori_loop(head_start, n, send_queries, 0)

    @pl.when(me == 0)
    def _():
        for j in range(2):
            for w in range(WMAX - 1):
                pltpu.make_async_copy(
                    caches[j].at[0, cached - WMAX + 1 + w],
                    wholes[j].at[pl.ds(w * BLK, BLK), pl.ds(0, HD)],
                    hrecv.at[j],
                ).start()

    row = lax.broadcasted_iota(jnp.int32, (BLK, WMAX * BLK), 0)
    col = lax.broadcasted_iota(jnp.int32, (BLK, WMAX * BLK), 1)
    late = col - (WMAX - 1) * BLK > row
    width = jnp.where(col < BLK, 3.0, jnp.where(col < 2 * BLK, 2.0, jnp.where(late, 99.0, 1.0)))
    thr[...] = width

    def window_part(h, blocks):
        span = wbuf[h, 0:1, 0:1]
        allowed = thr[...] <= span
        for b in blocks:
            q = qv[b * BLK : (b + 1) * BLK, columns(h)]
            k = kall[b * BLK : b * BLK + WMAX * BLK, columns(h)]
            v = vall[b * BLK : b * BLK + WMAX * BLK, columns(h)]
            s = jnp.where(allowed, nt_dot(q, k), MASKED)
            top = jnp.max(s, axis=1, keepdims=True)
            e = jnp.exp2((s - top) * SCALE2)
            total = jnp.sum(e, axis=1, keepdims=True)
            o = jnp.dot(e.astype(jnp.bfloat16), v, preferred_element_type=jnp.float32)
            owbuf[h, b * BLK : (b + 1) * BLK, :] = o / total
            lwbuf[h, b * BLK : (b + 1) * BLK, :] = jnp.broadcast_to(
                top * SCALE2 + jnp.log2(total), (BLK, HD)
            )

    for copy in local:
        copy.wait()

    diagonal = lax.broadcasted_iota(jnp.int32, (BLK, HD), 0) == lax.broadcasted_iota(
        jnp.int32, (BLK, HD), 1
    )
    stat_row = lax.broadcasted_iota(jnp.int32, (STAT, HD), 0)

    def far_part(i, carry):
        src = source(i)

        pltpu.make_async_copy(qbuf.at[i], qbuf.at[i], qrecv.at[i]).wait()
        stats = jnp.zeros((STAT, HD), jnp.float32)
        for b in range(nb):
            picks = [glob_ref[0, g] for g in range(GLOB)] + [
                rand_ref[0, src * nb + b, r] for r in range(RAND)
            ]
            k = jnp.concatenate([kcv[x] for x in picks], axis=0)
            v = jnp.concatenate([vcv[x] for x in picks], axis=0)
            s = nt_dot(qbuf[i, b * BLK : (b + 1) * BLK, :], k)
            top = jnp.max(s, axis=1, keepdims=True)
            e = jnp.exp2((s - top) * SCALE2)
            total = jnp.sum(e, axis=1, keepdims=True)
            o = jnp.dot(e.astype(jnp.bfloat16), v, preferred_element_type=jnp.float32)
            obuf[i, b * BLK : (b + 1) * BLK, :] = (o / total).astype(jnp.bfloat16)
            lse = top * SCALE2 + jnp.log2(total)
            line = jnp.sum(jnp.where(diagonal, lse, 0.0), axis=0, keepdims=True)
            for part in range(3):
                piece = line.astype(jnp.bfloat16).astype(jnp.float32)
                stats = jnp.where(stat_row == part * nb + b, piece, stats)
                line = line - piece
        obuf[i, nb * BLK : nb * BLK + STAT, :] = stats.astype(jnp.bfloat16)

        @pl.when(i > 0)
        def _():
            remote(obuf.at[i], ogbuf.at[i], osend, orecv.at[i], src).start()

        @pl.when(i == 0)
        def _():
            pltpu.make_async_copy(obuf.at[i], ogbuf.at[i], orecv.at[i]).start()
            pltpu.make_async_copy(wbuf.at[pl.ds(1, n - 1)], wbuf.at[pl.ds(1, n - 1)], wrecv).wait()

        turn = i - min(4, n // 2)

        @pl.when((turn == 0) & jnp.logical_not(edge) & ahead)
        def _():
            pltpu.make_async_copy(relay, relay, rrecv).wait()

        @pl.when((turn >= 0) & (turn < quarter // HD) & jnp.logical_not(edge) & ahead)
        def _():
            for j in range(2):
                remote(
                    relay.at[j, :, columns(turn)],
                    wholes[j].at[lead, columns(y * (quarter // HD) + turn)],
                    rsend,
                    hrecv.at[j],
                    (z + 1) * ny,
                ).start()

        @pl.when((i == 1 + lax.div(me, ny * 2)) & (me > 0))
        def _():
            for j in range(2):
                for w in range(WMAX - 1):
                    remote(
                        caches[j].at[0, cached - WMAX + 1 + w],
                        wholes[j].at[pl.ds(w * BLK, BLK), columns(me)],
                        tsend,
                        hrecv.at[j],
                        0,
                    ).start()

        window_part(src, range(WMAX - 1, nb))
        return carry

    lax.fori_loop(0, n, far_part, 0)

    for j, whole in enumerate((kall, vall)):
        pltpu.make_async_copy(whole.at[pl.ds(0, LEAD)], whole.at[pl.ds(0, LEAD)], hrecv.at[j]).wait()

    def join(i, carry):
        h = peer(i)
        window_part(h, range(WMAX - 1))
        pltpu.make_async_copy(ogbuf.at[i], ogbuf.at[i], orecv.at[i]).wait()
        stats = ogbuf[i, nb * BLK : nb * BLK + STAT, :].astype(jnp.float32)
        for b in range(nb):
            line = (stats[b : b + 1] + stats[nb + b : nb + b + 1]) + stats[2 * nb + b : 2 * nb + b + 1]
            far = jnp.sum(jnp.where(diagonal, line, 0.0), axis=1, keepdims=True)
            near = lwbuf[h, b * BLK : (b + 1) * BLK, :]
            share = 1.0 / (1.0 + jnp.exp2(near - far))
            ow = owbuf[h, b * BLK : (b + 1) * BLK, :]
            og = ogbuf[i, b * BLK : (b + 1) * BLK, :].astype(jnp.float32)
            fbuf[i, b * BLK : (b + 1) * BLK, :] = (ow + share * (og - ow)).astype(jnp.bfloat16)
        remote(fbuf.at[i], out_hbm.at[0, :, columns(h)], fsend, frecv, me, after).start()
        return carry

    lax.fori_loop(0, n, join, 0)

    pltpu.make_async_copy(wbuf.at[pl.ds(1, n - 1)], wbuf.at[pl.ds(1, n - 1)], wsend).wait()
    pltpu.make_async_copy(qbuf.at[pl.ds(1, n - 1)], qbuf.at[pl.ds(1, n - 1)], qsend).wait()
    pltpu.make_async_copy(obuf.at[pl.ds(1, n - 1)], obuf.at[pl.ds(1, n - 1)], osend).wait()
    pltpu.make_async_copy(fbuf, fbuf, fsend).wait()
    pltpu.make_async_copy(out_hbm.at[0], out_hbm.at[0], frecv).wait()

    @pl.when(jnp.logical_not(edge))
    def _():
        for j, whole in enumerate(wholes):
            pltpu.make_async_copy(whole.at[lead], whole.at[lead], hsend.at[j]).wait()

    @pl.when(edge & ahead)
    def _():
        for j in range(2):
            pltpu.make_async_copy(relay.at[j], relay.at[j], hsend.at[j]).wait()
        sent = kall.at[pl.ds(0, 2 * LEAD), pl.ds(0, (ny - 1) * quarter)]
        pltpu.make_async_copy(sent, sent, rsend).wait()

    @pl.when(jnp.logical_not(edge) & ahead)
    def _():
        pltpu.make_async_copy(relay, relay, rsend).wait()

    @pl.when(me > 0)
    def _():
        sent = kcv.at[pl.ds(0, 2 * (WMAX - 1))]
        pltpu.make_async_copy(sent, sent, tsend).wait()


def per_device(n, ny, sections, q, k, v, kc, vc, window, glob, rand):
    rows, wide = q.shape[1:]
    cached = kc.shape[1] // BLK
    kc, vc = (cache.reshape(1, cached, BLK, HD) for cache in (kc, vc))
    any_space = pl.BlockSpec(memory_space=pl.ANY)
    smem = pl.BlockSpec(memory_space=pltpu.SMEM)
    bf, f32, dma = jnp.bfloat16, jnp.float32, pltpu.SemaphoreType.DMA
    return pl.pallas_call(
        functools.partial(kernel, n, ny, sections),
        out_shape=jax.ShapeDtypeStruct(q.shape, bf),
        in_specs=[any_space] * 5 + [smem] * 3,
        out_specs=any_space,
        scratch_shapes=[
            pltpu.VMEM((rows, wide), bf),
            pltpu.VMEM((rows + LEAD, wide), bf),
            pltpu.VMEM((rows + LEAD, wide), bf),
            pltpu.VMEM((cached, BLK, HD), bf),
            pltpu.VMEM((cached, BLK, HD), bf),
            pltpu.VMEM((n, rows, HD), bf),
            pltpu.VMEM((n, rows + STAT, HD), bf),
            pltpu.VMEM((n, rows + STAT, HD), bf),
            pltpu.VMEM((n, rows, HD), f32),
            pltpu.VMEM((n, rows, HD), f32),
            pltpu.VMEM((n, rows, HD), bf),
            pltpu.VMEM((n, 8, HD), f32),
            pltpu.VMEM((2, LEAD, wide // ny), bf),
            pltpu.VMEM((BLK, WMAX * BLK), f32),
            dma((5,)),
            dma((n,)),
            dma((n,)),
            dma,
            dma,
            dma,
            dma,
            dma,
            dma,
            dma((2,)),
            dma((2,)),
            dma,
            dma,
            dma,
        ],
        compiler_params=pltpu.CompilerParams(
            collective_id=0, has_side_effects=True, vmem_limit_bytes=56 * 1024 * 1024
        ),
    )(q, k, v, kc, vc, window, glob, rand)


def solution(mesh):
    n, sections = mesh.shape["seq"], mesh.shape["section"]
    ny = math.gcd(n, 4)
    placed = (
        P("section", "seq", None),
        P("section", "seq", None),
        P("section", "seq", None),
        P("section", None, "seq"),
        P("section", None, "seq"),
        P("section", "seq"),
        P("section", None),
        P("section", None, None),
    )
    return jax.shard_map(
        functools.partial(per_device, n, ny, sections),
        mesh=mesh,
        in_specs=placed,
        out_specs=P("section", "seq", None),
        check_vma=False,
    )
```

```python
import functools
import math

import jax
import jax.numpy as jnp
from jax import lax
from jax.experimental import pallas as pl
from jax.experimental.pallas import tpu as pltpu
from jax.sharding import PartitionSpec as P

HD = 128
BLK = 64
WMAX = 3
GLOB = 2
RAND = 3
LEAD = (WMAX - 1) * BLK
STAT = 16

MESH = pl.DeviceIdType.MESH
SCALE2 = math.log2(math.e) / math.sqrt(HD)
MASKED = -1e30


def signed_step(j, size):
    half = lax.div(j + 1, 2)
    odd = lax.rem(j, 2)
    return lax.rem(half * (2 * odd - 1) + size, size)


def nt_dot(a, b):
    return lax.dot_general(a, b, (((1,), (1,)), ((), ())), preferred_element_type=jnp.float32)


def kernel(
    n,
    ny,
    sections,
    q_hbm,
    k_hbm,
    v_hbm,
    kc_hbm,
    vc_hbm,
    win_ref,
    glob_ref,
    rand_ref,
    out_hbm,
    qv,
    kall,
    vall,
    kcv,
    vcv,
    qbuf,
    obuf,
    ogbuf,
    owbuf,
    lwbuf,
    fbuf,
    wbuf,
    relay,
    thr,
    loc_sem,
    qrecv,
    orecv,
    qsend,
    osend,
    fsend,
    frecv,
    wsend,
    wrecv,
    hrecv,
    hsend,
    rsend,
    rrecv,
):
    nz = n // ny
    rows = q_hbm.shape[1]
    cached = kc_hbm.shape[1]
    nb = rows // BLK
    sec = lax.axis_index("section")
    me = lax.axis_index("seq")
    z, y = lax.div(me, ny), lax.rem(me, ny)

    def at(i, back):
        dz = signed_step(lax.rem(i, nz), nz)
        dy = signed_step(lax.div(i, nz), ny)
        if back:
            dz, dy = nz - dz, ny - dy
        return lax.rem(z + dz, nz) * ny + lax.rem(y + dy, ny)

    def peer(i):
        return at(i, False)

    def source(i):
        return at(i, True)

    def columns(h):
        return pl.ds(pl.multiple_of(h * HD, HD), HD)

    def remote(src, dst, send, recv, seq, section=None):
        where = {"section": sec if section is None else section, "seq": seq}
        return pltpu.make_async_remote_copy(
            src_ref=src, dst_ref=dst, send_sem=send, recv_sem=recv, device_id=where, device_id_type=MESH
        )

    after = lax.rem(sec + 1, sections)
    before = lax.rem(sec + sections - 1, sections)

    local = [
        pltpu.make_async_copy(q_hbm.at[0], qv, loc_sem.at[0]),
        pltpu.make_async_copy(k_hbm.at[0], kall.at[pl.ds(LEAD, rows)], loc_sem.at[1]),
        pltpu.make_async_copy(v_hbm.at[0], vall.at[pl.ds(LEAD, rows)], loc_sem.at[2]),
        pltpu.make_async_copy(kc_hbm.at[0], kcv, loc_sem.at[3]),
        pltpu.make_async_copy(vc_hbm.at[0], vcv, loc_sem.at[4]),
    ]
    for copy in local:
        copy.start()
    pltpu.make_async_copy(q_hbm.at[0, :, columns(me)], qbuf.at[0], qrecv.at[0]).start()

    wbuf[me] = jnp.full((8, HD), win_ref[0, 0].astype(jnp.float32))

    barrier = pltpu.get_barrier_semaphore()

    def greet(i, carry):
        pl.semaphore_signal(barrier, 1, device_id={"section": sec, "seq": peer(i)}, device_id_type=MESH)
        return carry

    lax.fori_loop(1, n, greet, 0)
    for other in (after, before):
        pl.semaphore_signal(barrier, 1, device_id={"section": other, "seq": me}, device_id_type=MESH)
    pl.semaphore_wait(barrier, n + 1)

    wide = q_hbm.shape[2]
    quarter = wide // ny
    lead = pl.ds(0, LEAD)
    last = pl.ds(rows - LEAD, LEAD)
    fresh = (k_hbm, v_hbm)
    wholes = (kall, vall)
    edge = y == ny - 1
    ahead = z < nz - 1

    parts = n // 2
    piece = wide // parts
    per = parts // ny

    plane = wbuf.at[pl.ds(pl.multiple_of(z * ny, ny), ny)]

    def send_window_y(i, carry):
        near = z * ny + lax.rem(y + i, ny)
        remote(wbuf.at[me], wbuf.at[me], wsend.at[0], wrecv.at[0], near).start()
        return carry

    def send_window_z(i, carry):
        far = lax.rem(z + i, nz) * ny + y
        remote(plane, plane, wsend.at[1], wrecv.at[1], far).start()
        return carry

    def tiles(count, sem):
        pltpu.make_async_copy(wbuf.at[pl.ds(0, count)], wbuf.at[pl.ds(0, count)], sem).wait()

    def send_queries(i, carry):
        p = peer(i)
        remote(q_hbm.at[0, :, columns(p)], qbuf.at[i], qsend, qrecv.at[i], p).start()
        at_part = i - 1
        part = pl.ds(pl.multiple_of(at_part * piece, HD), piece)
        column = lax.div(at_part, per)
        by_relay = edge & (column < ny - 1)

        @pl.when((at_part < parts) & by_relay & ahead)
        def _():
            held = pl.ds(pl.multiple_of(lax.rem(at_part, per) * piece, HD), piece)
            for j in range(2):
                remote(
                    fresh[j].at[0, last, part], relay.at[j, :, held], rsend, rrecv, z * ny + column
                ).start()

        @pl.when((at_part < parts) & jnp.logical_not(by_relay) & (me < n - 1))
        def _():
            for j in range(2):
                remote(
                    fresh[j].at[0, last, part], wholes[j].at[lead, part], hsend.at[j], hrecv.at[j], me + 1
                ).start()

        return carry

    head_start = min(9, n)
    lax.fori_loop(1, ny, send_window_y, 0)
    lax.fori_loop(1, head_start, send_queries, 0)
    tiles(ny - 1, wrecv.at[0])
    lax.fori_loop(1, nz, send_window_z, 0)
    lax.fori_loop(head_start, n, send_queries, 0)

    @pl.when(me == 0)
    def _():
        for whole in wholes:
            whole[lead, :] = jnp.zeros((LEAD, wide), jnp.bfloat16)

    row = lax.broadcasted_iota(jnp.int32, (BLK, WMAX * BLK), 0)
    col = lax.broadcasted_iota(jnp.int32, (BLK, WMAX * BLK), 1)
    late = col - (WMAX - 1) * BLK > row
    width = jnp.where(col < BLK, 3.0, jnp.where(col < 2 * BLK, 2.0, jnp.where(late, 99.0, 1.0)))
    for b in range(WMAX):
        unseen = jnp.where(me == 0, (WMAX - 1 - b) * BLK, 0)
        thr[b] = jnp.where(col < unseen, 99.0, width)

    def window_part(h, blocks):
        span = wbuf[h, 0:1, 0:1]
        for b in blocks:
            allowed = thr[min(b, WMAX - 1)] <= span
            q = qv[b * BLK : (b + 1) * BLK, columns(h)]
            k = kall[b * BLK : b * BLK + WMAX * BLK, columns(h)]
            v = vall[b * BLK : b * BLK + WMAX * BLK, columns(h)]
            s = jnp.where(allowed, nt_dot(q, k), MASKED)
            top = jnp.max(s, axis=1, keepdims=True)
            e = jnp.exp2((s - top) * SCALE2)
            total = jnp.sum(e, axis=1, keepdims=True)
            o = jnp.dot(e.astype(jnp.bfloat16), v, preferred_element_type=jnp.float32)
            owbuf[h, b * BLK : (b + 1) * BLK, :] = o / total
            lwbuf[h, b * BLK : (b + 1) * BLK, :] = jnp.broadcast_to(
                top * SCALE2 + jnp.log2(total), (BLK, HD)
            )

    for copy in local:
        copy.wait()

    diagonal = lax.broadcasted_iota(jnp.int32, (BLK, HD), 0) == lax.broadcasted_iota(
        jnp.int32, (BLK, HD), 1
    )
    stat_row = lax.broadcasted_iota(jnp.int32, (STAT, HD), 0)

    span_here = win_ref[0, 0].astype(jnp.float32)

    def far_chunk(i, src, opening):
        stats = jnp.zeros((STAT, HD), jnp.float32)
        for b in range(nb):
            picks = [glob_ref[0, g] for g in range(GLOB)] + [
                rand_ref[r, 0, src * nb + b] for r in range(RAND)
            ]
            extra = WMAX - 1 - b if opening and b < WMAX - 1 else 0
            picks += [cached - extra + w for w in range(extra)]
            k = jnp.concatenate([kcv[x] for x in picks], axis=0)
            v = jnp.concatenate([vcv[x] for x in picks], axis=0)
            s = nt_dot(qbuf[i, b * BLK : (b + 1) * BLK, :], k)
            if extra:
                place = lax.broadcasted_iota(jnp.int32, s.shape, 1) - (GLOB + RAND) * BLK
                least = jnp.where(place < 0, 0.0, jnp.where(place < BLK, 3.0, 2.0))
                s = jnp.where(least <= span_here, s, MASKED)
            top = jnp.max(s, axis=1, keepdims=True)
            e = jnp.exp2((s - top) * SCALE2)
            total = jnp.sum(e, axis=1, keepdims=True)
            o = jnp.dot(e.astype(jnp.bfloat16), v, preferred_element_type=jnp.float32)
            obuf[i, b * BLK : (b + 1) * BLK, :] = (o / total).astype(jnp.bfloat16)
            lse = top * SCALE2 + jnp.log2(total)
            line = jnp.sum(jnp.where(diagonal, lse, 0.0), axis=0, keepdims=True)
            for part in range(3):
                piece = line.astype(jnp.bfloat16).astype(jnp.float32)
                stats = jnp.where(stat_row == part * nb + b, piece, stats)
                line = line - piece
        obuf[i, nb * BLK : nb * BLK + STAT, :] = stats.astype(jnp.bfloat16)

    def far_part(i, carry):
        src = source(i)

        pltpu.make_async_copy(qbuf.at[i], qbuf.at[i], qrecv.at[i]).wait()
        @pl.when(src == 0)
        def _():
            far_chunk(i, src, True)

        @pl.when(src > 0)
        def _():
            far_chunk(i, src, False)

        @pl.when(i > 0)
        def _():
            remote(obuf.at[i], ogbuf.at[i], osend, orecv.at[i], src).start()

        @pl.when(i == 0)
        def _():
            pltpu.make_async_copy(obuf.at[i], ogbuf.at[i], orecv.at[i]).start()
            tiles(n - ny, wrecv.at[1])

        turn = i - min(4, n // 2)

        @pl.when((turn == 0) & jnp.logical_not(edge) & ahead)
        def _():
            pltpu.make_async_copy(relay, relay, rrecv).wait()

        @pl.when((turn >= 0) & (turn < quarter // HD) & jnp.logical_not(edge) & ahead)
        def _():
            for j in range(2):
                remote(
                    relay.at[j, :, columns(turn)],
                    wholes[j].at[lead, columns(y * (quarter // HD) + turn)],
                    rsend,
                    hrecv.at[j],
                    (z + 1) * ny,
                ).start()

        window_part(src, range(WMAX - 1, nb))
        return carry

    lax.fori_loop(0, n, far_part, 0)

    @pl.when(me > 0)
    def _():
        for j, whole in enumerate(wholes):
            pltpu.make_async_copy(whole.at[lead], whole.at[lead], hrecv.at[j]).wait()


    def join(i, carry):
        h = peer(i)
        window_part(h, range(WMAX - 1))
        pltpu.make_async_copy(ogbuf.at[i], ogbuf.at[i], orecv.at[i]).wait()
        stats = ogbuf[i, nb * BLK : nb * BLK + STAT, :].astype(jnp.float32)
        for b in range(nb):
            line = (stats[b : b + 1] + stats[nb + b : nb + b + 1]) + stats[2 * nb + b : 2 * nb + b + 1]
            far = jnp.sum(jnp.where(diagonal, line, 0.0), axis=1, keepdims=True)
            near = lwbuf[h, b * BLK : (b + 1) * BLK, :]
            share = 1.0 / (1.0 + jnp.exp2(near - far))
            ow = owbuf[h, b * BLK : (b + 1) * BLK, :]
            og = ogbuf[i, b * BLK : (b + 1) * BLK, :].astype(jnp.float32)
            fbuf[i, b * BLK : (b + 1) * BLK, :] = (ow + share * (og - ow)).astype(jnp.bfloat16)
        remote(fbuf.at[i], out_hbm.at[0, :, columns(h)], fsend, frecv, me, after).start()
        return carry

    lax.fori_loop(0, n, join, 0)

    tiles(ny - 1, wsend.at[0])
    tiles(n - ny, wsend.at[1])
    pltpu.make_async_copy(qbuf.at[pl.ds(1, n - 1)], qbuf.at[pl.ds(1, n - 1)], qsend).wait()
    pltpu.make_async_copy(obuf.at[pl.ds(1, n - 1)], obuf.at[pl.ds(1, n - 1)], osend).wait()
    pltpu.make_async_copy(fbuf, fbuf, fsend).wait()
    pltpu.make_async_copy(out_hbm.at[0], out_hbm.at[0], frecv).wait()

    @pl.when(jnp.logical_not(edge))
    def _():
        for j, whole in enumerate(wholes):
            pltpu.make_async_copy(whole.at[lead], whole.at[lead], hsend.at[j]).wait()

    @pl.when(edge & ahead)
    def _():
        for j in range(2):
            pltpu.make_async_copy(relay.at[j], relay.at[j], hsend.at[j]).wait()
        sent = kall.at[pl.ds(0, 2 * LEAD), pl.ds(0, (ny - 1) * quarter)]
        pltpu.make_async_copy(sent, sent, rsend).wait()

    @pl.when(jnp.logical_not(edge) & ahead)
    def _():
        pltpu.make_async_copy(relay, relay, rsend).wait()


def per_device(n, ny, sections, q, k, v, kc, vc, window, glob, rand):
    rows, wide = q.shape[1:]
    cached = kc.shape[1] // BLK
    kc, vc = (cache.reshape(1, cached, BLK, HD) for cache in (kc, vc))
    any_space = pl.BlockSpec(memory_space=pl.ANY)
    smem = pl.BlockSpec(memory_space=pltpu.SMEM)
    bf, f32, dma = jnp.bfloat16, jnp.float32, pltpu.SemaphoreType.DMA
    return pl.pallas_call(
        functools.partial(kernel, n, ny, sections),
        out_shape=jax.ShapeDtypeStruct(q.shape, bf),
        in_specs=[any_space] * 5 + [smem] * 3,
        out_specs=any_space,
        scratch_shapes=[
            pltpu.VMEM((rows, wide), bf),
            pltpu.VMEM((rows + LEAD, wide), bf),
            pltpu.VMEM((rows + LEAD, wide), bf),
            pltpu.VMEM((cached, BLK, HD), bf),
            pltpu.VMEM((cached, BLK, HD), bf),
            pltpu.VMEM((n, rows, HD), bf),
            pltpu.VMEM((n, rows + STAT, HD), bf),
            pltpu.VMEM((n, rows + STAT, HD), bf),
            pltpu.VMEM((n, rows, HD), f32),
            pltpu.VMEM((n, rows, HD), f32),
            pltpu.VMEM((n, rows, HD), bf),
            pltpu.VMEM((n, 8, HD), f32),
            pltpu.VMEM((2, LEAD, wide // ny), bf),
            pltpu.VMEM((WMAX, BLK, WMAX * BLK), f32),
            dma((5,)),
            dma((n,)),
            dma((n,)),
            dma,
            dma,
            dma,
            dma,
            dma((2,)),
            dma((2,)),
            dma((2,)),
            dma((2,)),
            dma,
            dma,
        ],
        compiler_params=pltpu.CompilerParams(
            collective_id=0, has_side_effects=True, vmem_limit_bytes=56 * 1024 * 1024
        ),
    )(q, k, v, kc, vc, window, glob, jnp.transpose(rand, (2, 0, 1)))


def solution(mesh):
    n, sections = mesh.shape["seq"], mesh.shape["section"]
    ny = math.gcd(n, 4)
    placed = (
        P("section", "seq", None),
        P("section", "seq", None),
        P("section", "seq", None),
        P("section", None, "seq"),
        P("section", None, "seq"),
        P("section", "seq"),
        P("section", None),
        P("section", None, None),
    )
    return jax.shard_map(
        functools.partial(per_device, n, ny, sections),
        mesh=mesh,
        in_specs=placed,
        out_specs=P("section", "seq", None),
        check_vma=False,
    )
```

```python
import functools
import math

import jax
import jax.numpy as jnp
from jax import lax
from jax.experimental import pallas as pl
from jax.experimental.pallas import tpu as pltpu
from jax.sharding import PartitionSpec as P

HD = 128
BLK = 64
WMAX = 3
GLOB = 2
RAND = 3
LEAD = (WMAX - 1) * BLK
STAT = 16

MESH = pl.DeviceIdType.MESH
SCALE2 = math.log2(math.e) / math.sqrt(HD)
MASKED = -1e30


def signed_step(j, size):
    half = lax.div(j + 1, 2)
    odd = lax.rem(j, 2)
    return lax.rem(half * (2 * odd - 1) + size, size)


def nt_dot(a, b):
    return lax.dot_general(a, b, (((1,), (1,)), ((), ())), preferred_element_type=jnp.float32)


def kernel(
    n,
    ny,
    sections,
    q_hbm,
    k_hbm,
    v_hbm,
    kc_hbm,
    vc_hbm,
    win_ref,
    glob_ref,
    rand_ref,
    out_hbm,
    qv,
    kall,
    vall,
    kcv,
    vcv,
    qbuf,
    obuf,
    ogbuf,
    owbuf,
    lwbuf,
    fbuf,
    wbuf,
    relay,
    thr,
    loc_sem,
    qrecv,
    orecv,
    qsend,
    osend,
    fsend,
    frecv,
    wsend,
    wrecv,
    hrecv,
    hsend,
    rsend,
    rrecv,
):
    nz = n // ny
    rows = q_hbm.shape[1]
    cached = kc_hbm.shape[1]
    nb = rows // BLK
    sec = lax.axis_index("section")
    me = lax.axis_index("seq")
    z, y = lax.div(me, ny), lax.rem(me, ny)

    def at(i, back):
        dz = signed_step(lax.rem(i, nz), nz)
        dy = signed_step(lax.div(i, nz), ny)
        if back:
            dz, dy = nz - dz, ny - dy
        return lax.rem(z + dz, nz) * ny + lax.rem(y + dy, ny)

    def peer(i):
        return at(i, False)

    def source(i):
        return at(i, True)

    def columns(h):
        return pl.ds(pl.multiple_of(h * HD, HD), HD)

    def remote(src, dst, send, recv, seq, section=None):
        where = {"section": sec if section is None else section, "seq": seq}
        return pltpu.make_async_remote_copy(
            src_ref=src, dst_ref=dst, send_sem=send, recv_sem=recv, device_id=where, device_id_type=MESH
        )

    after = lax.rem(sec + 1, sections)
    before = lax.rem(sec + sections - 1, sections)

    local = [
        pltpu.make_async_copy(q_hbm.at[0], qv, loc_sem.at[0]),
        pltpu.make_async_copy(k_hbm.at[0], kall.at[pl.ds(LEAD, rows)], loc_sem.at[1]),
        pltpu.make_async_copy(v_hbm.at[0], vall.at[pl.ds(LEAD, rows)], loc_sem.at[2]),
        pltpu.make_async_copy(kc_hbm.at[0], kcv, loc_sem.at[3]),
        pltpu.make_async_copy(vc_hbm.at[0], vcv, loc_sem.at[4]),
    ]
    for copy in local:
        copy.start()
    pltpu.make_async_copy(q_hbm.at[0, :, columns(me)], qbuf.at[0], qrecv.at[0]).start()

    wbuf[me] = jnp.full((8, HD), win_ref[0, 0].astype(jnp.float32))

    barrier = pltpu.get_barrier_semaphore()

    def greet(i, carry):
        pl.semaphore_signal(barrier, 1, device_id={"section": sec, "seq": peer(i)}, device_id_type=MESH)
        return carry

    lax.fori_loop(1, n, greet, 0)
    for other in (after, before):
        pl.semaphore_signal(barrier, 1, device_id={"section": other, "seq": me}, device_id_type=MESH)
    pl.semaphore_wait(barrier, n + 1)

    wide = q_hbm.shape[2]
    quarter = wide // ny
    lead = pl.ds(0, LEAD)
    last = pl.ds(rows - LEAD, LEAD)
    fresh = (k_hbm, v_hbm)
    wholes = (kall, vall)
    edge = y == ny - 1
    ahead = z < nz - 1

    parts = n // 2
    piece = wide // parts
    per = parts // ny

    plane = wbuf.at[pl.ds(pl.multiple_of(z * ny, ny), ny)]

    def send_window_y(i, carry):
        near = z * ny + lax.rem(y + i, ny)
        remote(wbuf.at[me], wbuf.at[me], wsend.at[0], wrecv.at[0], near).start()
        return carry

    def send_window_z(i, carry):
        far = lax.rem(z + i, nz) * ny + y
        remote(plane, plane, wsend.at[1], wrecv.at[1], far).start()
        return carry

    def tiles(count, sem):
        pltpu.make_async_copy(wbuf.at[pl.ds(0, count)], wbuf.at[pl.ds(0, count)], sem).wait()

    def send_queries(i, carry):
        p = peer(i)
        remote(q_hbm.at[0, :, columns(p)], qbuf.at[i], qsend, qrecv.at[i], p).start()
        at_part = i - 1
        part = pl.ds(pl.multiple_of(at_part * piece, HD), piece)
        column = lax.div(at_part, per)
        by_relay = edge & (column < ny - 1)

        @pl.when((at_part < parts) & by_relay & ahead)
        def _():
            held = pl.ds(pl.multiple_of(lax.rem(at_part, per) * piece, HD), piece)
            for j in range(2):
                remote(
                    fresh[j].at[0, last, part], relay.at[j, :, held], rsend, rrecv, z * ny + column
                ).start()

        @pl.when((at_part < parts) & jnp.logical_not(by_relay) & (me < n - 1))
        def _():
            for j in range(2):
                remote(
                    fresh[j].at[0, last, part], wholes[j].at[lead, part], hsend.at[j], hrecv.at[j], me + 1
                ).start()

        return carry

    head_start = min(9, n)
    lax.fori_loop(1, ny, send_window_y, 0)
    lax.fori_loop(1, head_start, send_queries, 0)
    tiles(ny - 1, wrecv.at[0])
    lax.fori_loop(1, nz, send_window_z, 0)
    lax.fori_loop(head_start, n, send_queries, 0)

    @pl.when(me == 0)
    def _():
        for whole in wholes:
            whole[lead, :] = jnp.zeros((LEAD, wide), jnp.bfloat16)

    row = lax.broadcasted_iota(jnp.int32, (BLK, WMAX * BLK), 0)
    col = lax.broadcasted_iota(jnp.int32, (BLK, WMAX * BLK), 1)
    late = col - (WMAX - 1) * BLK > row
    width = jnp.where(col < BLK, 3.0, jnp.where(col < 2 * BLK, 2.0, jnp.where(late, 99.0, 1.0)))
    for b in range(WMAX):
        unseen = jnp.where(me == 0, (WMAX - 1 - b) * BLK, 0)
        thr[b] = jnp.where(col < unseen, 99.0, width)

    def window_part(h, blocks):
        span = wbuf[h, 0:1, 0:1]
        for b in blocks:
            allowed = thr[min(b, WMAX - 1)] <= span
            q = qv[b * BLK : (b + 1) * BLK, columns(h)]
            k = kall[b * BLK : b * BLK + WMAX * BLK, columns(h)]
            v = vall[b * BLK : b * BLK + WMAX * BLK, columns(h)]
            s = jnp.where(allowed, nt_dot(q, k), MASKED)
            top = jnp.max(s, axis=1, keepdims=True)
            e = jnp.exp2((s - top) * SCALE2)
            total = jnp.sum(e, axis=1, keepdims=True)
            o = jnp.dot(e.astype(jnp.bfloat16), v, preferred_element_type=jnp.float32)
            owbuf[h, b * BLK : (b + 1) * BLK, :] = o / total
            lwbuf[h, b * BLK : (b + 1) * BLK, :] = jnp.broadcast_to(
                top * SCALE2 + jnp.log2(total), (BLK, HD)
            )

    for copy in local:
        copy.wait()

    diagonal = lax.broadcasted_iota(jnp.int32, (BLK, HD), 0) == lax.broadcasted_iota(
        jnp.int32, (BLK, HD), 1
    )
    stat_row = lax.broadcasted_iota(jnp.int32, (STAT, HD), 0)

    span_here = win_ref[0, 0].astype(jnp.float32)

    def far_chunk(i, src, opening):
        stats = jnp.zeros((STAT, HD), jnp.float32)
        for b in range(nb):
            picks = [glob_ref[0, g] for g in range(GLOB)] + [
                rand_ref[r, 0, src * nb + b] for r in range(RAND)
            ]
            extra = WMAX - 1 - b if opening and b < WMAX - 1 else 0
            picks += [cached - extra + w for w in range(extra)]
            k = jnp.concatenate([kcv[x] for x in picks], axis=0)
            v = jnp.concatenate([vcv[x] for x in picks], axis=0)
            s = nt_dot(qbuf[i, b * BLK : (b + 1) * BLK, :], k)
            if extra:
                place = lax.broadcasted_iota(jnp.int32, s.shape, 1) - (GLOB + RAND) * BLK
                least = jnp.where(place < 0, 0.0, jnp.where(place < BLK, 3.0, 2.0))
                s = jnp.where(least <= span_here, s, MASKED)
            top = jnp.max(s, axis=1, keepdims=True)
            e = jnp.exp2((s - top) * SCALE2)
            total = jnp.sum(e, axis=1, keepdims=True)
            o = jnp.dot(e.astype(jnp.bfloat16), v, preferred_element_type=jnp.float32)
            obuf[i, b * BLK : (b + 1) * BLK, :] = (o / total).astype(jnp.bfloat16)
            lse = top * SCALE2 + jnp.log2(total)
            line = jnp.sum(jnp.where(diagonal, lse, 0.0), axis=0, keepdims=True)
            for part in range(3):
                piece = line.astype(jnp.bfloat16).astype(jnp.float32)
                stats = jnp.where(stat_row == part * nb + b, piece, stats)
                line = line - piece
        obuf[i, nb * BLK : nb * BLK + STAT, :] = stats.astype(jnp.bfloat16)

    def far_part(i, carry):
        src = source(i)

        pltpu.make_async_copy(qbuf.at[i], qbuf.at[i], qrecv.at[i]).wait()
        @pl.when(src == 0)
        def _():
            far_chunk(i, src, True)

        @pl.when(src > 0)
        def _():
            far_chunk(i, src, False)

        @pl.when(i > 0)
        def _():
            remote(obuf.at[i], ogbuf.at[i], osend, orecv.at[i], src).start()

        @pl.when(i == 0)
        def _():
            pltpu.make_async_copy(obuf.at[i], ogbuf.at[i], orecv.at[i]).start()
            tiles(n - ny, wrecv.at[1])

        turn = i - min(2, n // 2)

        @pl.when((turn == 0) & jnp.logical_not(edge) & ahead)
        def _():
            pltpu.make_async_copy(relay, relay, rrecv).wait()

        @pl.when((turn >= 0) & (turn < quarter // HD) & jnp.logical_not(edge) & ahead)
        def _():
            for j in range(2):
                remote(
                    relay.at[j, :, columns(turn)],
                    wholes[j].at[lead, columns(y * (quarter // HD) + turn)],
                    rsend,
                    hrecv.at[j],
                    (z + 1) * ny,
                ).start()

        window_part(src, range(WMAX - 1, nb))
        return carry

    lax.fori_loop(0, n, far_part, 0)

    @pl.when(me > 0)
    def _():
        for j, whole in enumerate(wholes):
            pltpu.make_async_copy(whole.at[lead], whole.at[lead], hrecv.at[j]).wait()


    def join(i, carry):
        h = peer(i)
        window_part(h, range(WMAX - 1))
        pltpu.make_async_copy(ogbuf.at[i], ogbuf.at[i], orecv.at[i]).wait()
        stats = ogbuf[i, nb * BLK : nb * BLK + STAT, :].astype(jnp.float32)
        for b in range(nb):
            line = (stats[b : b + 1] + stats[nb + b : nb + b + 1]) + stats[2 * nb + b : 2 * nb + b + 1]
            far = jnp.sum(jnp.where(diagonal, line, 0.0), axis=1, keepdims=True)
            near = lwbuf[h, b * BLK : (b + 1) * BLK, :]
            share = 1.0 / (1.0 + jnp.exp2(near - far))
            ow = owbuf[h, b * BLK : (b + 1) * BLK, :]
            og = ogbuf[i, b * BLK : (b + 1) * BLK, :].astype(jnp.float32)
            fbuf[i, b * BLK : (b + 1) * BLK, :] = (ow + share * (og - ow)).astype(jnp.bfloat16)
        remote(fbuf.at[i], out_hbm.at[0, :, columns(h)], fsend, frecv, me, after).start()
        return carry

    lax.fori_loop(0, n, join, 0)

    tiles(ny - 1, wsend.at[0])
    tiles(n - ny, wsend.at[1])
    pltpu.make_async_copy(qbuf.at[pl.ds(1, n - 1)], qbuf.at[pl.ds(1, n - 1)], qsend).wait()
    pltpu.make_async_copy(obuf.at[pl.ds(1, n - 1)], obuf.at[pl.ds(1, n - 1)], osend).wait()
    pltpu.make_async_copy(fbuf, fbuf, fsend).wait()
    pltpu.make_async_copy(out_hbm.at[0], out_hbm.at[0], frecv).wait()

    @pl.when(jnp.logical_not(edge))
    def _():
        for j, whole in enumerate(wholes):
            pltpu.make_async_copy(whole.at[lead], whole.at[lead], hsend.at[j]).wait()

    @pl.when(edge & ahead)
    def _():
        for j in range(2):
            pltpu.make_async_copy(relay.at[j], relay.at[j], hsend.at[j]).wait()
        sent = kall.at[pl.ds(0, 2 * LEAD), pl.ds(0, (ny - 1) * quarter)]
        pltpu.make_async_copy(sent, sent, rsend).wait()

    @pl.when(jnp.logical_not(edge) & ahead)
    def _():
        pltpu.make_async_copy(relay, relay, rsend).wait()


def per_device(n, ny, sections, q, k, v, kc, vc, window, glob, rand):
    rows, wide = q.shape[1:]
    cached = kc.shape[1] // BLK
    kc, vc = (cache.reshape(1, cached, BLK, HD) for cache in (kc, vc))
    any_space = pl.BlockSpec(memory_space=pl.ANY)
    smem = pl.BlockSpec(memory_space=pltpu.SMEM)
    bf, f32, dma = jnp.bfloat16, jnp.float32, pltpu.SemaphoreType.DMA
    return pl.pallas_call(
        functools.partial(kernel, n, ny, sections),
        out_shape=jax.ShapeDtypeStruct(q.shape, bf),
        in_specs=[any_space] * 5 + [smem] * 3,
        out_specs=any_space,
        scratch_shapes=[
            pltpu.VMEM((rows, wide), bf),
            pltpu.VMEM((rows + LEAD, wide), bf),
            pltpu.VMEM((rows + LEAD, wide), bf),
            pltpu.VMEM((cached, BLK, HD), bf),
            pltpu.VMEM((cached, BLK, HD), bf),
            pltpu.VMEM((n, rows, HD), bf),
            pltpu.VMEM((n, rows + STAT, HD), bf),
            pltpu.VMEM((n, rows + STAT, HD), bf),
            pltpu.VMEM((n, rows, HD), f32),
            pltpu.VMEM((n, rows, HD), f32),
            pltpu.VMEM((n, rows, HD), bf),
            pltpu.VMEM((n, 8, HD), f32),
            pltpu.VMEM((2, LEAD, wide // ny), bf),
            pltpu.VMEM((WMAX, BLK, WMAX * BLK), f32),
            dma((5,)),
            dma((n,)),
            dma((n,)),
            dma,
            dma,
            dma,
            dma,
            dma((2,)),
            dma((2,)),
            dma((2,)),
            dma((2,)),
            dma,
            dma,
        ],
        compiler_params=pltpu.CompilerParams(
            collective_id=0, has_side_effects=True, vmem_limit_bytes=56 * 1024 * 1024
        ),
    )(q, k, v, kc, vc, window, glob, jnp.transpose(rand, (2, 0, 1)))


def solution(mesh):
    n, sections = mesh.shape["seq"], mesh.shape["section"]
    ny = math.gcd(n, 4)
    placed = (
        P("section", "seq", None),
        P("section", "seq", None),
        P("section", "seq", None),
        P("section", None, "seq"),
        P("section", None, "seq"),
        P("section", "seq"),
        P("section", None),
        P("section", None, None),
    )
    return jax.shard_map(
        functools.partial(per_device, n, ny, sections),
        mesh=mesh,
        in_specs=placed,
        out_specs=P("section", "seq", None),
        check_vma=False,
    )
```
